256 devices in a mesh: segment: 4 (over z_hi), dp: 4 (over x), expert: 16 (over y, z_lo, core).
Axes of the slice: x: 4, y: 4, z: 8 (z_hi: 4, z_lo: 2; z = z_hi * 2 + z_lo), core: 2. Of those that a mesh axis runs over, the one named last changes fastest.
Arguments:
- fwd_inputs: bfloat16 [4, 4096, 2048], P('segment', ('dp', 'expert')), may hold values from -17 to 17
- fwd_routes: int32 [4, 4096, 8], P('segment', ('dp', 'expert')), may hold values from 0 to 127, as said below
- fwd_weights: float32 [4, 4096, 8], P('segment', ('dp', 'expert')), may hold values from 0.2 to 0.6
- bwd_inputs: bfloat16 [4, 4096, 2048], P('segment', ('dp', 'expert')), may hold values from -17 to 17
- bwd_cotangent: bfloat16 [4, 4096, 2048], P('segment', ('dp', 'expert')), may hold values from -6 to 6
- bwd_routes: int32 [4, 4096, 8], P('segment', ('dp', 'expert')), may hold values from 0 to 127, as said below
- bwd_weights: float32 [4, 4096, 8], P('segment', ('dp', 'expert')), may hold values from 0.2 to 0.6
- norm_gain: float32 [4, 2048], P('segment'), may hold values from 0.5 to 2
- w_gate: bfloat16 [4, 128, 2048, 384], P('segment', ('dp', 'expert')), may hold values from -0.125 to 0.125
- w_up: bfloat16 [4, 128, 2048, 384], P('segment', ('dp', 'expert')), may hold values from -0.125 to 0.125
- w_down: bfloat16 [4, 128, 384, 2048], P('segment', ('dp', 'expert')), may hold values from -0.3125 to 0.3125
Outputs:
- next_forward: bfloat16 [4, 4096, 2048], P('segment', ('dp', 'expert'))
- prev_grad: bfloat16 [4, 4096, 2048], P('segment', ('dp', 'expert'))
The draws below stay inside these ranges and needn't reach their ends.
Inputs may be any that keep to these rules, and one draw needn't show every extreme that they name: `fwd_routes`: each row names 8 different experts. Among the rows of one device no expert is named more than 5 times, and in each section one expert is named exactly 5 times on every device of that section. `bwd_routes`: each row names 8 different experts. Among the rows of one device no expert is named more than 5 times, and in each section one expert is named exactly 5 times on every device of that section.
All inputs are finite; a program needn't handle non-finite values.
Results may differ from the reference program's by a relative error of at most 0.0059.
Values may be sent and summed in bfloat16 or wider, within the bound.
No kernel may reach another device: no remote copies, remote signals or barrier semaphores. Data moves between devices by JAX's collectives and lax.ppermute only.
A program may use at most 128 MiB of HBM per device.

```python
import math
import jax
import jax.numpy as jnp
from jax import lax

D = 2048
TOPK = 8
FFE = 384
TOK_DEV = 64
SEGMENTS = 4
EXPERTS = 128
TOKENS = 4096
CAP = 5
N_DP = 4
N_EXPERT = 16


def route_table(base_key):
    blocks_count = TOKENS // TOK_DEV
    entries = TOK_DEV * TOPK
    tickets = EXPERTS * CAP

    def one_segment(segment_key):
        first_key, second_key, third_key, fourth_key = jax.random.split(segment_key, 4)
        expert_bias = jax.random.randint(first_key, (EXPERTS,), 0, 48)
        hot_expert = jax.random.randint(second_key, (), 0, EXPERTS)
        rename = jax.random.permutation(third_key, EXPERTS).astype(jnp.int32)
        owners = jnp.arange(tickets, dtype=jnp.int32) // CAP

        def one_block(block_key):
            noise_key, order_key = jax.random.split(block_key)
            priority = jax.random.randint(noise_key, (tickets,), 0, 32) + expert_bias[owners] + 1000 * (owners == hot_expert).astype(jnp.int32)
            ranked = priority * tickets + jnp.arange(tickets, dtype=jnp.int32)
            unused, chosen = lax.top_k(ranked, entries)
            chosen = jnp.sort(chosen)
            experts_list = rename[chosen // CAP]
            layout = experts_list.reshape(TOPK, TOK_DEV).T
            row_order = jax.random.permutation(order_key, TOK_DEV)
            return layout[row_order]
        tables = jax.vmap(one_block)(jax.random.split(fourth_key, blocks_count))
        return tables.reshape(TOKENS, TOPK)
    return jax.vmap(one_segment)(jax.random.split(base_key, SEGMENTS)).astype(jnp.int32)


def activation_field(base_key):
    first_key, second_key, third_key = jax.random.split(base_key, 3)
    shape_full = (SEGMENTS, TOKENS, D)
    basis = jnp.clip(jax.random.normal(first_key, shape_full, jnp.float32), -4.0, 4.0)
    row_scale = jnp.exp(jax.random.uniform(second_key, (SEGMENTS, TOKENS, 1), jnp.float32, -0.7, 0.7))
    column_scale = jnp.exp(jax.random.uniform(third_key, (D,), jnp.float32, -0.7, 0.7))
    return (basis * row_scale * column_scale).astype(jnp.bfloat16)


def draw_fwd_routes(key, part):
    return route_table(jax.random.fold_in(key, 11))


def draw_bwd_routes(key, part):
    return route_table(jax.random.fold_in(key, 23))


def draw_fwd_inputs(key, part):
    return activation_field(jax.random.fold_in(key, 37))


def draw_bwd_inputs(key, part):
    return activation_field(jax.random.fold_in(key, 41))


def block_levels(stream_key, extent, cuts, least, top_value):
    loudness, own = 1.0, jax.random.fold_in(stream_key, 6)
    for axis_at, shards_of in cuts:
        draws = jnp.exp(jax.random.uniform(jax.random.fold_in(own, axis_at), (shards_of,), jnp.float32, least / len(cuts), top_value / len(cuts)))
        loudness = loudness * jnp.repeat(draws, extent[axis_at] // shards_of).reshape([-1 if axis == axis_at else 1 for axis in range(len(extent))])
    return loudness


def noise(own_key, shape, width, most, cuts=(), kind=jnp.bfloat16):
    gain = block_levels(own_key, shape, cuts, -0.22, 0.18) if cuts else 1.0
    result = jax.random.normal(own_key, shape, jnp.float32) * width * gain
    return jnp.minimum(jnp.maximum(result, -most), most).astype(kind)


def setup_inputs(seed: int = 0) -> dict:
    streams_of = jax.random.split(jax.random.key(seed), 12)
    return {
        "fwd_inputs": draw_fwd_inputs(jax.random.fold_in(streams_of[11], 71), 0),
        "fwd_routes": draw_fwd_routes(jax.random.fold_in(streams_of[11], 71), 0),
        "fwd_weights": jnp.clip(0.2 + 0.400000021 * jax.random.uniform(streams_of[2], (SEGMENTS, TOKENS, TOPK), jnp.float32) ** block_levels(streams_of[2], (SEGMENTS, TOKENS, TOPK), ((0, 4), (1, 64)), -0.2, 0.2), 0.2, 0.6),
        "bwd_inputs": draw_bwd_inputs(jax.random.fold_in(streams_of[11], 71), 0),
        "bwd_cotangent": noise(streams_of[4], (SEGMENTS, TOKENS, D), 1.0, 6.0, ((0, 4), (1, 64))),
        "bwd_routes": draw_bwd_routes(jax.random.fold_in(streams_of[11], 71), 0),
        "bwd_weights": jnp.clip(0.2 + 0.400000021 * jax.random.uniform(streams_of[6], (SEGMENTS, TOKENS, TOPK), jnp.float32) ** block_levels(streams_of[6], (SEGMENTS, TOKENS, TOPK), ((0, 4), (1, 64)), -0.2, 0.2), 0.2, 0.6),
        "norm_gain": jnp.clip(jnp.exp(math.log(2.0) - 1.3862944 * jax.random.uniform(streams_of[7], (SEGMENTS, D), jnp.float32) ** block_levels(streams_of[7], (SEGMENTS, D), ((0, 4),), -0.2, 0.2)), 0.5, 2.0),
        "w_gate": noise(streams_of[8], (SEGMENTS, EXPERTS, D, FFE), D ** -0.5, 0.125, ((0, 4), (1, 64))),
        "w_up": noise(streams_of[9], (SEGMENTS, EXPERTS, D, FFE), D ** -0.5, 0.125, ((0, 4), (1, 64))),
        "w_down": noise(streams_of[10], (SEGMENTS, EXPERTS, FFE, D), FFE ** -0.5, 0.3125, ((0, 4), (1, 64))),
    }


EPSILON = 1e-06

def normalize(inputs, norm_scale):
    values = inputs.astype(jnp.float32)
    inv_rms = lax.rsqrt(lax.optimization_barrier(jnp.mean(values * values, axis=-1, keepdims=True)) + EPSILON)
    return ((values * inv_rms * norm_scale).astype(jnp.bfloat16), values, inv_rms)

def expert_rows(normed_rows, back_rows, cotangent_rows, gate_mat, up_mat, down_mat):
    gate_proj = jnp.dot(normed_rows, gate_mat, preferred_element_type=jnp.float32)
    up_proj = jnp.dot(normed_rows, up_mat, preferred_element_type=jnp.float32)
    activated = (gate_proj * jax.nn.sigmoid(gate_proj) * up_proj).astype(jnp.bfloat16)
    out_rows = jnp.dot(activated, down_mat, preferred_element_type=jnp.float32).astype(jnp.bfloat16)
    gate_back = jnp.dot(back_rows, gate_mat, preferred_element_type=jnp.float32)
    up_back = jnp.dot(back_rows, up_mat, preferred_element_type=jnp.float32)
    back_hidden = jnp.dot(cotangent_rows, down_mat.T, preferred_element_type=jnp.float32)
    sigmoid_gate = jax.nn.sigmoid(gate_back)
    d_gate = (back_hidden * up_back * sigmoid_gate * (1.0 + gate_back * (1.0 - sigmoid_gate))).astype(jnp.bfloat16)
    d_up = (back_hidden * gate_back * sigmoid_gate).astype(jnp.bfloat16)
    d_normed = (jnp.dot(d_gate, gate_mat.T, preferred_element_type=jnp.float32) + jnp.dot(d_up, up_mat.T, preferred_element_type=jnp.float32)).astype(jnp.bfloat16)
    return (out_rows, d_normed)

def section(fwd_inputs, fwd_routes, fwd_weights, bwd_inputs, bwd_cotangent, bwd_routes, bwd_weights, norm_scale, w_gate, w_up, w_down):
    normed_fwd = normalize(fwd_inputs, norm_scale)[0]
    normed_bwd, back_values, back_rms = normalize(bwd_inputs, norm_scale)
    entries = TOKENS * TOPK
    most_rows = N_DP * N_EXPERT * CAP
    fwd_flat = fwd_routes.reshape(-1)
    bwd_flat = bwd_routes.reshape(-1)
    fwd_factors = fwd_weights.reshape(-1)
    bwd_factors = bwd_weights.reshape(-1)

    def visit(carry, member):
        expert_id, gate_mat, up_mat, down_mat = member
        acc_fwd, acc_bwd = carry
        fwd_index = jnp.nonzero(fwd_flat == expert_id, size=most_rows, fill_value=entries)[0].astype(jnp.int32)
        bwd_index = jnp.nonzero(bwd_flat == expert_id, size=most_rows, fill_value=entries)[0].astype(jnp.int32)
        fwd_clip = jnp.minimum(fwd_index, entries - 1)
        bwd_clip = jnp.minimum(bwd_index, entries - 1)
        fwd_token = fwd_clip // TOPK
        bwd_token = bwd_clip // TOPK
        out_rows, d_rows = expert_rows(normed_fwd[fwd_token], normed_bwd[bwd_token], bwd_cotangent[bwd_token], gate_mat, up_mat, down_mat)
        fwd_scale = jnp.where(fwd_index < entries, fwd_factors[fwd_clip], jnp.zeros_like(fwd_factors[fwd_clip]))
        bwd_scale = jnp.where(bwd_index < entries, bwd_factors[bwd_clip], jnp.zeros_like(bwd_factors[bwd_clip]))
        acc_fwd = acc_fwd.at[fwd_token].add(out_rows.astype(jnp.float32) * fwd_scale[:, None])
        acc_bwd = acc_bwd.at[bwd_token].add(d_rows.astype(jnp.float32) * bwd_scale[:, None])
        return ((acc_fwd, acc_bwd), None)
    start = (jnp.zeros((TOKENS, D), jnp.float32), jnp.zeros((TOKENS, D), jnp.float32))
    members = (jnp.arange(EXPERTS, dtype=jnp.int32), w_gate, w_up, w_down)
    (combined, norm_grad), unused = lax.scan(visit, start, members)
    section_out = (fwd_inputs.astype(jnp.float32) + combined).astype(jnp.bfloat16)
    scaled = norm_scale * norm_grad
    section_grad = (bwd_cotangent.astype(jnp.float32) + back_rms * scaled - back_values * back_rms ** 3 * lax.optimization_barrier(jnp.mean(back_values * scaled, axis=-1, keepdims=True))).astype(jnp.bfloat16)
    return (section_out, section_grad)

def reference(fwd_inputs, fwd_routes, fwd_weights, bwd_inputs, bwd_cotangent, bwd_routes, bwd_weights, norm_gain, w_gate, w_up, w_down):
    outs_list = []
    grads_list = []
    for segment_id in range(SEGMENTS):
        section_out, section_grad = section(fwd_inputs[segment_id], fwd_routes[segment_id], fwd_weights[segment_id], bwd_inputs[segment_id], bwd_cotangent[segment_id], bwd_routes[segment_id], bwd_weights[segment_id], norm_gain[segment_id], w_gate[segment_id], w_up[segment_id], w_down[segment_id])
        outs_list.append(section_out)
        grads_list.append(section_grad)
    next_forward = jnp.roll(jnp.stack(outs_list), 1, axis=0)
    prev_grad = jnp.roll(jnp.stack(grads_list), -1, axis=0)
    return (next_forward, prev_grad)
```

```python
import jax
import jax.numpy as jnp
from jax import lax
from jax.experimental import pallas as pl
from jax.experimental.pallas import tpu as pltpu
from jax.sharding import PartitionSpec as P

EPSILON = 1e-06
BF = jnp.bfloat16
F32 = jnp.float32
SLOTS = 5
ROWS = 4
NN = (((1,), (0,)), ((), ()))
NT = (((1,), (1,)), ((), ()))


def dot(left, right, dims=NN):
    return lax.dot_general(left, right, dims, preferred_element_type=F32)


def iota(shape, axis):
    return lax.broadcasted_iota(jnp.int32, shape, axis)


def onehot(mask):
    return jnp.where(mask, 1.0, 0.0).astype(BF)


def slot_marks(routes, experts):
    tokens, top = routes.shape
    lanes = iota((tokens, experts), 1)
    member = jnp.zeros((tokens, experts), F32)
    for k in range(top):
        member = jnp.where(routes[:, k : k + 1] == lanes, 1.0, member)
    upto = onehot(iota((tokens, tokens), 1) <= iota((tokens, tokens), 0))
    return (dot(upto, member.astype(BF)) * member).astype(BF)


def normalize(inputs, norm_scale):
    values = inputs.astype(F32)
    inv_rms = lax.rsqrt(jnp.mean(values * values, axis=-1, keepdims=True) + EPSILON)
    return values * inv_rms * norm_scale, values, inv_rms


def pack_kernel(experts, fwd, bwd, cot, fwd_routes, bwd_routes, gain, out, tile, sems):
    tokens, width = fwd.shape
    quarter = width // ROWS
    wide = width + quarter
    rows = experts * ROWS
    copies = []

    def masks(routes):
        marks = slot_marks(routes[...], experts)
        spread = onehot(iota((rows, experts), 0) // ROWS == iota((rows, experts), 1))
        table = dot(spread, jnp.concatenate([marks] * ROWS, axis=0), NT)
        place = iota((rows, ROWS * tokens), 0) % ROWS
        last = onehot((table == SLOTS) & (place == iota((rows, ROWS * tokens), 1) // tokens))
        main = onehot(table[:, :tokens] == (place[:, :tokens] + 1).astype(F32))
        return main, last

    def emit(index, values, main, last):
        for q in range(ROWS):
            cols = pl.ds(q * quarter, quarter)
            tile[index, :, cols] = dot(main, values[:, q * quarter : (q + 1) * quarter]).astype(BF)
        stacked = jnp.concatenate(
            [values[:, q * quarter : (q + 1) * quarter] for q in range(ROWS)], axis=0
        )
        tile[index, :, pl.ds(width, quarter)] = dot(last, stacked).astype(BF)
        copy = pltpu.make_async_copy(
            tile.at[index], out.at[:, pl.ds(index * wide, wide)], sems.at[index]
        )
        copy.start()
        copies.append(copy)

    main, last = masks(bwd_routes)
    emit(2, cot[...], main, last)
    emit(1, normalize(bwd[...], gain[...])[0].astype(BF), main, last)
    main, last = masks(fwd_routes)
    emit(0, normalize(fwd[...], gain[...])[0].astype(BF), main, last)
    for copy in copies:
        copy.wait()


def expert_kernel(
    arrived, w_gate, w_up, w_down, out, got, gate, up, down, rows_in, outs, lasts, back, sems
):
    local, width, hidden = w_gate.shape
    quarter = width // ROWS
    wide = width + quarter
    total = arrived.shape[0]
    span = local * ROWS
    groups = total // span
    bulk = groups * ROWS
    loads = []
    for a in range(3):
        loads.append(
            pltpu.make_async_copy(arrived.at[:, pl.ds(a * wide, wide)], got.at[a], sems.at[a])
        )
    loads.append(pltpu.make_async_copy(w_gate, gate, sems.at[3]))
    loads.append(pltpu.make_async_copy(w_up, up, sems.at[4]))
    loads.append(pltpu.make_async_copy(w_down, down, sems.at[5]))
    for load in loads:
        load.start()

    def per_array(a):
        def per_expert(e, carry):
            m = iota((bulk, total), 0)
            pick = onehot(iota((bulk, total), 1) == (m // ROWS) * span + e * ROWS + m % ROWS)
            tail = onehot(iota((bulk, total), 1) == (m % groups) * span + e * ROWS + m // groups)

            for q in range(ROWS):
                cols = pl.ds(q * quarter, quarter)
                rows_in[a, e, pl.ds(0, bulk), cols] = dot(pick, got[a, :, cols]).astype(BF)
            rest = dot(tail, got[a, :, pl.ds(width, quarter)]).astype(BF)
            for q in range(ROWS):
                rows_in[a, e, pl.ds(bulk, groups), pl.ds(q * quarter, quarter)] = rest[
                    q * groups : (q + 1) * groups
                ]
            return carry

        lax.fori_loop(0, local, per_expert, 0)

    def put(b, e, q, values):
        values = values.astype(BF)
        cols = pl.ds(q * quarter, quarter)
        outs[b, pl.ds(e * bulk, bulk), cols] = values[:bulk]
        lasts[b, pl.ds((e * ROWS + q) * groups, groups), :] = values[bulk:]

    def finish(b):
        side = local * bulk
        i = iota((total, side), 0)
        c = iota((total, side), 1)
        m = c % bulk
        spread = onehot(i == (m // ROWS) * span + (c // bulk) * ROWS + m % ROWS)
        tail = onehot(i == (c % groups) * span + c // groups)
        for q in range(ROWS):
            cols = pl.ds(q * quarter, quarter)
            back[b, :, cols] = dot(spread, outs[b, :, cols]).astype(BF)
        back[b, :, pl.ds(width, quarter)] = dot(tail, lasts[b]).astype(BF)
        copy = pltpu.make_async_copy(
            back.at[b], out.at[:, pl.ds(b * wide, wide)], sems.at[6 + b]
        )
        copy.start()
        return copy

    def forward(e, carry):
        x = rows_in[0, e]
        g = dot(x, gate[e])
        u = dot(x, up[e])
        act = (g * jax.nn.sigmoid(g) * u).astype(BF)
        for q in range(ROWS):
            put(0, e, q, dot(act, down[e, :, pl.ds(q * quarter, quarter)]))
        return carry

    def backward(e, carry):
        x = rows_in[1, e]
        g = dot(x, gate[e])
        u = dot(x, up[e])
        h = dot(rows_in[2, e], down[e], NT)
        s = jax.nn.sigmoid(g)
        d_gate = (h * u * s * (1.0 + g * (1.0 - s))).astype(BF)
        d_up = (h * g * s).astype(BF)
        for q in range(ROWS):
            part = pl.ds(q * quarter, quarter)
            put(1, e, q, dot(d_gate, gate[e, part, :], NT) + dot(d_up, up[e, part, :], NT))
        return carry

    loads[0].wait()
    per_array(0)
    for load in loads[3:]:
        load.wait()
    lax.fori_loop(0, local, forward, 0)
    first = finish(0)
    loads[1].wait()
    per_array(1)
    loads[2].wait()
    per_array(2)
    lax.fori_loop(0, local, backward, 0)
    second = finish(1)
    first.wait()
    second.wait()


def weighted_sum(experts, returned, routes, weights):
    tokens, top = routes.shape
    wide = returned.shape[1]
    quarter = wide // (ROWS + 1)
    width = quarter * ROWS
    rows = experts * ROWS
    marks = slot_marks(routes, experts)
    spread = onehot(iota((rows, experts), 0) // ROWS == iota((rows, experts), 1))
    table = dot(marks, spread, NT)
    column = iota((tokens, rows), 1)
    factor = jnp.zeros((tokens, rows), F32)
    for k in range(top):
        factor = jnp.where(routes[:, k : k + 1] == column // ROWS, weights[:, k : k + 1], factor)
    place = column % ROWS

    def split(values):
        high = values.astype(BF)
        return high, (values - high.astype(F32)).astype(BF)

    main = jnp.concatenate(
        split(jnp.where(table == (place + 1).astype(F32), factor, 0.0)), axis=0
    )
    tails = []
    for q in range(ROWS):
        tails.extend(split(jnp.where((table == SLOTS) & (place == q), factor, 0.0)))
    extra = dot(jnp.concatenate(tails, axis=0), returned[:, pl.ds(width, quarter)])
    pieces = []
    for q in range(ROWS):
        piece = dot(main, returned[:, pl.ds(q * quarter, quarter)])
        at = 2 * q * tokens
        pieces.append(
            (piece[:tokens] + piece[tokens:])
            + (extra[at : at + tokens] + extra[at + tokens : at + 2 * tokens])
        )
    return jnp.concatenate(pieces, axis=1)


def forward_kernel(experts, returned, inputs, routes, weights, out):
    combined = weighted_sum(experts, returned, routes[...], weights[...])
    out[...] = (inputs[...].astype(F32) + combined).astype(BF)


def backward_kernel(experts, returned, inputs, cot, routes, weights, gain, out):
    norm_grad = weighted_sum(experts, returned, routes[...], weights[...])
    norm_scale = gain[...]
    _, values, inv_rms = normalize(inputs[...], norm_scale)
    scaled = norm_scale * norm_grad
    mean = jnp.mean(values * scaled, axis=-1, keepdims=True)
    out[...] = (
        cot[...].astype(F32) + inv_rms * scaled - values * (inv_rms * inv_rms * inv_rms) * mean
    ).astype(BF)


def from_behind(value, axis, steps):
    count = lax.axis_size(axis)
    pairs = [(source, (source + steps) % count) for source in range(count)]
    return lax.ppermute(value, axis, pairs)


def body(
    fwd_inputs,
    fwd_routes,
    fwd_weights,
    bwd_inputs,
    bwd_cotangent,
    bwd_routes,
    bwd_weights,
    norm_gain,
    w_gate,
    w_up,
    w_down,
):
    _, tokens, width = fwd_inputs.shape
    local = w_gate.shape[1]
    hidden = w_gate.shape[3]
    group = lax.axis_size("dp") * lax.axis_size("expert")
    experts = local * group
    rows = experts * ROWS
    quarter = width // ROWS
    wide = width + quarter
    bulk = group * ROWS
    vmem = pl.BlockSpec(memory_space=pltpu.VMEM)
    hbm = pl.BlockSpec(memory_space=pl.ANY)
    limit = pltpu.CompilerParams(vmem_limit_bytes=60 * 1024 * 1024)

    packed = pl.pallas_call(
        lambda *refs: pack_kernel(experts, *refs),
        out_shape=jax.ShapeDtypeStruct((rows, 3 * wide), BF),
        in_specs=[vmem] * 6,
        out_specs=hbm,
        scratch_shapes=[pltpu.VMEM((3, rows, wide), BF), pltpu.SemaphoreType.DMA((3,))],
        compiler_params=limit,
        name="pack",
    )(fwd_inputs[0], bwd_inputs[0], bwd_cotangent[0], fwd_routes[0], bwd_routes[0], norm_gain)

    arrived = lax.all_to_all(packed, ("dp", "expert"), split_axis=0, concat_axis=0, tiled=True)

    worked = pl.pallas_call(
        expert_kernel,
        out_shape=jax.ShapeDtypeStruct((rows, 2 * wide), BF),
        in_specs=[hbm] * 4,
        out_specs=hbm,
        scratch_shapes=[
            pltpu.VMEM((3, rows, wide), BF),
            pltpu.VMEM((local, width, hidden), BF),
            pltpu.VMEM((local, width, hidden), BF),
            pltpu.VMEM((local, hidden, width), BF),
            pltpu.VMEM((3, local, bulk + group, width), BF),
            pltpu.VMEM((2, local * bulk, width), BF),
            pltpu.VMEM((2, local * ROWS * group, quarter), BF),
            pltpu.VMEM((2, rows, wide), BF),
            pltpu.SemaphoreType.DMA((8,)),
        ],
        compiler_params=limit,
        name="experts",
    )(arrived, w_gate[0], w_up[0], w_down[0])

    returned = lax.all_to_all(worked, ("dp", "expert"), split_axis=0, concat_axis=0, tiled=True)

    def whole(array):
        return pl.BlockSpec(array.shape, lambda i: (0,) * array.ndim)

    def combine(kernel, part, *rest, name):
        return pl.pallas_call(
            lambda *refs: kernel(experts, *refs),
            out_shape=jax.ShapeDtypeStruct((tokens, width), BF),
            grid=(1,),
            in_specs=[pl.BlockSpec((rows, wide), lambda i: (0, part))] + [whole(r) for r in rest],
            out_specs=pl.BlockSpec((tokens, width), lambda i: (0, 0)),
            compiler_params=limit,
            name=name,
        )(returned, *rest)

    section_out = combine(
        forward_kernel, 0, fwd_inputs[0], fwd_routes[0], fwd_weights[0], name="forward"
    )
    section_grad = combine(
        backward_kernel,
        1,
        bwd_inputs[0],
        bwd_cotangent[0],
        bwd_routes[0],
        bwd_weights[0],
        norm_gain,
        name="backward",
    )
    next_forward = from_behind(section_out[None], "segment", 1)
    prev_grad = from_behind(section_grad[None], "segment", -1)
    return (next_forward, prev_grad)


def solution(mesh):
    token = P("segment", ("dp", "expert"), None)
    weight = P("segment", ("dp", "expert"), None, None)
    return jax.shard_map(
        body,
        mesh=mesh,
        in_specs=(token,) * 7 + (P("segment", None),) + (weight,) * 3,
        out_specs=(token, token),
        check_vma=False,
    )
```

```python
import jax
import jax.numpy as jnp
from jax import lax
from jax.experimental import pallas as pl
from jax.experimental.pallas import tpu as pltpu
from jax.sharding import PartitionSpec as P

EPSILON = 1e-06
BF = jnp.bfloat16
F32 = jnp.float32
SLOTS = 5
ROWS = 4
NN = (((1,), (0,)), ((), ()))
NT = (((1,), (1,)), ((), ()))
TN = (((0,), (0,)), ((), ()))


def dot(left, right, dims=NN):
    return lax.dot_general(left, right, dims, preferred_element_type=F32)


def iota(shape, axis):
    return lax.broadcasted_iota(jnp.int32, shape, axis)


def onehot(mask):
    return jnp.where(mask, 1.0, 0.0).astype(BF)


def slot_marks(routes, experts):
    top, tokens = routes.shape
    ids = iota((experts, tokens), 0)
    member = jnp.zeros((experts, tokens), F32)
    for k in range(top):
        member = jnp.where(routes[k : k + 1] == ids, 1.0, member)
    upto = onehot(iota((tokens, tokens), 0) <= iota((tokens, tokens), 1))
    return (dot(member.astype(BF), upto) * member).astype(BF)


def spread_rows(experts):
    rows = experts * ROWS
    return onehot(iota((rows, experts), 0) // ROWS == iota((rows, experts), 1))


def normalize(inputs, norm_scale):
    values = inputs.astype(F32)
    inv_rms = lax.rsqrt(jnp.mean(values * values, axis=-1, keepdims=True) + EPSILON)
    return values * inv_rms * norm_scale, values, inv_rms


def sub(shape):
    return iota(shape, 0) % (2 * ROWS)


def pack_kernel(experts, fwd, bwd, cot, fwd_routes, bwd_routes, gain, out, tile, sems):
    tokens, width = fwd.shape
    quarter = width // ROWS
    rows = experts * ROWS
    copies = []

    def send(at, values):
        cols = pl.ds(at * quarter, quarter)
        tile[:, cols] = values.astype(BF)
        copy = pltpu.make_async_copy(tile.at[:, cols], out.at[:, cols], sems.at[at])
        copy.start()
        copies.append(copy)

    fwd_marks = slot_marks(fwd_routes[...], experts)
    bwd_marks = slot_marks(bwd_routes[...], experts)
    i = iota((rows, experts), 0) // (2 * ROWS)
    e = iota((rows, experts), 1)
    marks = jnp.concatenate([fwd_marks, bwd_marks], axis=1)
    table = [dot(onehot(e == 2 * i + odd), marks) for odd in range(2)]
    pair = (rows, 2 * tokens)
    slot = (sub(pair) % ROWS + 1).astype(F32)
    low = sub(pair) < ROWS
    is_fwd = iota(pair, 1) < tokens
    fwd_rows = normalize(fwd[...], gain[...])[0].astype(BF)
    bwd_rows = normalize(bwd[...], gain[...])[0].astype(BF)
    cot_rows = cot[...]
    both = jnp.concatenate([fwd_rows, bwd_rows], axis=0)
    picks = [
        onehot((table[0] == slot) & (low == is_fwd)),
        onehot((table[1] == slot) & (low != is_fwd)),
    ]
    for block in range(2):
        for q in range(ROWS):
            part = slice(q * quarter, (q + 1) * quarter)
            send(block * ROWS + q, dot(picks[block], both[:, part]))
    crossed = jnp.where(low, table[1], table[0])
    crossed = onehot((crossed == slot) & jnp.logical_not(is_fwd))
    cots = jnp.concatenate([jnp.zeros_like(cot_rows), cot_rows], axis=0)
    for q in range(ROWS):
        part = slice(q * quarter, (q + 1) * quarter)
        send(2 * ROWS + q, dot(crossed, cots[:, part]))
    stacked = [
        jnp.concatenate([v[:, q * quarter : (q + 1) * quarter] for q in range(ROWS)], axis=0)
        for v in (fwd_rows, bwd_rows, cot_rows)
    ]
    spread = spread_rows(experts)
    four = (rows, ROWS * tokens)
    mine = iota(four, 0) % ROWS == iota(four, 1) // tokens
    for a, marks in enumerate((fwd_marks, bwd_marks, bwd_marks)):
        if a < 2:
            wide_table = dot(spread, jnp.concatenate([marks] * ROWS, axis=1))
            last = onehot((wide_table == SLOTS) & mine)
        send(3 * ROWS + a, dot(last, stacked[a]))
    for copy in copies:
        copy.wait()


def prepare_kernel(experts, *refs):
    for routes, weights, out in zip(refs[0:2], refs[2:4], refs[4:6]):
        top, tokens = routes.shape
        rows = experts * ROWS
        routes = routes[...]
        weights = weights[...]
        table = dot(spread_rows(experts), slot_marks(routes, experts))
        row = iota((rows, tokens), 0)
        owner = row // ROWS
        place = row % ROWS
        factor = jnp.zeros((rows, tokens), F32)
        for k in range(top):
            factor = jnp.where(routes[k : k + 1] == owner, weights[k : k + 1], factor)
        high = factor.astype(BF).astype(F32)
        eye = onehot(iota((rows, rows), 0) == iota((rows, rows), 1))
        at = 0
        for half in (high, factor - high):
            picked = jnp.where(table == (place + 1).astype(F32), half, 0.0).astype(BF)
            out[pl.ds(at, tokens), :] = dot(picked, eye, TN).astype(BF)
            at += tokens
        for q in range(ROWS):
            for half in (high, factor - high):
                picked = jnp.where((table == SLOTS) & (place == q), half, 0.0).astype(BF)
                out[pl.ds(at, tokens), :] = dot(picked, eye, TN).astype(BF)
                at += tokens


def tiles_of(values):
    grouped = values.reshape(values.shape[0] // 16, 2, 8, values.shape[1])
    return grouped[:, 0], grouped[:, 1]


def turn(values):
    return pltpu.roll(values, ROWS, 1)


def is_low(values):
    return iota(values.shape, 1) < ROWS


def half_rows(values, upper):
    even, odd = tiles_of(values)
    if upper:
        joined = jnp.where(is_low(even), turn(even), odd)
    else:
        joined = jnp.where(is_low(even), even, turn(odd))
    return joined.reshape(values.shape[0] // 2, values.shape[1])


def weave(lower, upper):
    shape = (lower.shape[0] // 8, 8, lower.shape[1])
    lower = lower.reshape(shape)
    upper = upper.reshape(shape)
    even = jnp.where(is_low(lower), lower, turn(upper))
    odd = jnp.where(is_low(lower), turn(lower), upper)
    return jnp.stack([even, odd], axis=1).reshape(2 * shape[0] * 8, shape[2])


def expert_kernel(
    arrived, w_gate, w_up, w_down, out, x, ends, gate_up, down, gu, h, act, grad, lasts, tile,
    in_sems, out_sems,
):
    local, width, hidden = w_gate.shape
    quarter = width // ROWS
    total = arrived.shape[0]
    groups = total // (local * ROWS)
    bulk = groups * ROWS
    loads = [pltpu.make_async_copy(arrived.at[:, pl.ds(3 * width, 3 * quarter)], ends, in_sems.at[0])]
    for block in range(3):
        loads.append(
            pltpu.make_async_copy(
                arrived.at[:, pl.ds(block * width, width)],
                x.at[block, pl.ds(0, total), :],
                in_sems.at[1 + block],
            )
        )
    weights = []
    for e in range(local):
        weights.append(
            pltpu.make_async_copy(w_gate.at[e], gate_up.at[e, :, pl.ds(0, hidden)], in_sems.at[4 + 3 * e])
        )
        weights.append(
            pltpu.make_async_copy(w_up.at[e], gate_up.at[e, :, pl.ds(hidden, hidden)], in_sems.at[5 + 3 * e])
        )
        weights.append(
            pltpu.make_async_copy(w_down.at[e], down.at[pl.ds(e * hidden, hidden), :], in_sems.at[6 + 3 * e])
        )
    for load in (
        loads[0], loads[1], weights[0], weights[1], loads[2], weights[3], weights[4], loads[3],
        weights[2], weights[5],
    ):
        load.start()

    c = iota((total, total), 1)
    r = iota((total, total), 0)
    where_from = (r % groups) * (local * ROWS) + r // groups
    loads[0].wait()
    rest = dot(onehot(c == where_from), ends[...]).astype(BF)
    for a, e, block, place in (
        (0, 0, 0, 0), (1, 0, 0, 1), (1, 1, 1, 0), (0, 1, 1, 1), (2, 1, 2, 0), (2, 0, 2, 1),
    ):
        for q in range(ROWS):
            at = (e * ROWS + q) * groups
            x[block, pl.ds(total + place * groups, groups), pl.ds(q * quarter, quarter)] = rest[
                at : at + groups, a * quarter : (a + 1) * quarter
            ]

    step = 2 * hidden // 3
    for load in (loads[1], weights[0], weights[1], loads[2], weights[3], weights[4]):
        load.wait()

    def gate_up_part(n, carry):
        e, cols = n // 3, pl.ds(pl.multiple_of((n % 3) * step, step), step)
        gu[e, :, cols] = dot(x[e], gate_up[e, :, cols])
        return carry

    lax.fori_loop(0, 3 * local, gate_up_part, 0)
    for load in (loads[3], weights[2], weights[5]):
        load.wait()

    def hidden_part(n, carry):
        cols = pl.ds(pl.multiple_of(n * step, step), step)
        h[:, cols] = dot(x[2], down[cols, :], NT)
        return carry

    lax.fori_loop(0, 3, hidden_part, 0)

    for e in range(local):
        def take(ref_values, forward):
            upper = forward == (e == 1)
            main = half_rows(ref_values[:total], upper)
            at = total + groups * int(upper)
            return jnp.concatenate([main, ref_values[at : at + groups]], axis=0)

        for n in range(3):
            cols = slice(n * hidden // 3, (n + 1) * hidden // 3)
            at = n * hidden // 3
            g_all = gu[e, :, pl.ds(at, hidden // 3)]
            u_all = gu[e, :, pl.ds(hidden + at, hidden // 3)]
            g = take(g_all, True)
            u = take(u_all, True)
            act[e, :, cols] = (g * jax.nn.sigmoid(g) * u).astype(BF)
            g = take(g_all, False)
            u = take(u_all, False)
            b = take(h[:, pl.ds(e * hidden + at, hidden // 3)], False)
            s = jax.nn.sigmoid(g)
            grad[e, :, cols] = (b * u * s * (1.0 + g * (1.0 - s))).astype(BF)
            grad[e, :, pl.ds(hidden + at, hidden // 3)] = (b * g * s).astype(BF)

    copies = []

    def ship(at, count):
        cols = pl.ds(at * quarter, count * quarter)
        copy = pltpu.make_async_copy(tile.at[:, cols], out.at[:, cols], out_sems.at[at])
        copy.start()
        copies.append(copy)

    for a in range(2):
        for q in range(ROWS):
            part = pl.ds(q * quarter, quarter)
            if a == 0:
                o = [dot(act[e], down[pl.ds(e * hidden, hidden), part]) for e in range(local)]
            else:
                o = [dot(grad[e], gate_up[e, part, :], NT) for e in range(local)]
            tile[:, pl.ds((a * ROWS + q) * quarter, quarter)] = weave(o[0][:bulk], o[1][:bulk]).astype(BF)
            for e in range(local):
                lasts[pl.ds((e * ROWS + q) * groups, groups), pl.ds(a * quarter, quarter)] = o[e][
                    bulk:
                ].astype(BF)
            ship(a * ROWS + q, 1)
    where_to = (c % groups) * (local * ROWS) + c // groups
    tile[:, pl.ds(2 * width, 2 * quarter)] = dot(onehot(r == where_to), lasts[...]).astype(BF)
    ship(2 * ROWS, 2)
    for copy in copies:
        copy.wait()


def weighted_sum(part, loads, matrix, tile):
    tokens = matrix.shape[0] // (2 + 2 * ROWS)
    quarter = tile.shape[1] // (2 * ROWS + 2)
    pieces = []
    for q in range(ROWS):
        at = part * ROWS + q
        loads[at].wait()
        piece = dot(matrix[pl.ds(0, 2 * tokens), :], tile[:, pl.ds(at * quarter, quarter)])
        pieces.append(piece[:tokens] + piece[tokens:])
    at = 2 * ROWS + part
    loads[at].wait()
    extra = dot(
        matrix[pl.ds(2 * tokens, 2 * ROWS * tokens), :], tile[:, pl.ds(at * quarter, quarter)]
    )
    for q in range(ROWS):
        at = 2 * q * tokens
        pieces[q] += extra[at : at + tokens] + extra[at + tokens : at + 2 * tokens]
    return jnp.concatenate(pieces, axis=1)


def combine_kernel(*refs):
    (returned, hbm_others, outs, tile, others, sems) = (
        refs[0], refs[1:7], refs[7:9], refs[9], refs[10:16], refs[16],
    )
    quarter = tile.shape[1] // (2 * ROWS + 2)
    chunks = 2 * ROWS + 2
    loads = [
        pltpu.make_async_copy(
            returned.at[:, pl.ds(at * quarter, quarter)],
            tile.at[:, pl.ds(at * quarter, quarter)],
            sems.at[at],
        )
        for at in range(chunks)
    ]
    more = [
        pltpu.make_async_copy(source, target, sems.at[chunks + i])
        for i, (source, target) in enumerate(zip(hbm_others, others))
    ]
    bwd_matrix, fwd_matrix, bwd_inputs, cot, fwd_inputs, gain = others
    half = list(range(ROWS, 2 * ROWS)) + [2 * ROWS + 1]
    rest = list(range(ROWS)) + [2 * ROWS]
    order = [more[0]] + [loads[at] for at in half] + more[2:4] + [more[5], more[1]]
    for load in order + [loads[at] for at in rest] + [more[4]]:
        load.start()
    more[0].wait()
    norm_grad = weighted_sum(1, loads, bwd_matrix, tile)
    for i in (2, 3, 5):
        more[i].wait()
    norm_scale = gain[...]
    _, values, inv_rms = normalize(bwd_inputs[...], norm_scale)
    scaled = norm_scale * norm_grad
    mean = jnp.mean(values * scaled, axis=-1, keepdims=True)
    outs[1][...] = (
        cot[...].astype(F32) + inv_rms * scaled - values * (inv_rms * inv_rms * inv_rms) * mean
    ).astype(BF)
    more[1].wait()
    combined = weighted_sum(0, loads, fwd_matrix, tile)
    more[4].wait()
    outs[0][...] = (fwd_inputs[...].astype(F32) + combined).astype(BF)


def from_behind(value, axis, steps):
    count = lax.axis_size(axis)
    pairs = [(source, (source + steps) % count) for source in range(count)]
    return lax.ppermute(value, axis, pairs)


def body(
    fwd_inputs,
    fwd_routes,
    fwd_weights,
    bwd_inputs,
    bwd_cotangent,
    bwd_routes,
    bwd_weights,
    norm_gain,
    w_gate,
    w_up,
    w_down,
):
    _, tokens, width = fwd_inputs.shape
    local = w_gate.shape[1]
    hidden = w_gate.shape[3]
    group = lax.axis_size("dp") * lax.axis_size("expert")
    experts = local * group
    rows = experts * ROWS
    quarter = width // ROWS
    wide = width + quarter
    bulk = group * ROWS
    vmem = pl.BlockSpec(memory_space=pltpu.VMEM)
    hbm = pl.BlockSpec(memory_space=pl.ANY)
    limit = pltpu.CompilerParams(vmem_limit_bytes=65_000_000)
    fwd_routes = fwd_routes[0].T
    bwd_routes = bwd_routes[0].T
    fwd_weights = fwd_weights[0].T
    bwd_weights = bwd_weights[0].T

    def cost(flops, moved):
        return pl.CostEstimate(flops=int(flops), bytes_accessed=int(moved), transcendentals=0)

    def exchange(packed):
        return lax.all_to_all(packed, ("dp", "expert"), split_axis=0, concat_axis=0, tiled=True)

    packed = pl.pallas_call(
        lambda *refs: pack_kernel(experts, *refs),
        out_shape=jax.ShapeDtypeStruct((rows, 3 * wide), BF),
        in_specs=[vmem] * 6,
        out_specs=hbm,
        scratch_shapes=[
            pltpu.VMEM((rows, 3 * wide), BF),
            pltpu.SemaphoreType.DMA((3 * (ROWS + 1),)),
        ],
        compiler_params=limit,
        cost_estimate=cost(9e9, 9e6),
        name="pack",
    )(fwd_inputs[0], bwd_inputs[0], bwd_cotangent[0], fwd_routes, bwd_routes, norm_gain)
    arrived = exchange(packed)
    matrix_shape = jax.ShapeDtypeStruct(((2 + 2 * ROWS) * tokens, rows), BF)
    fwd_matrix, bwd_matrix = pl.pallas_call(
        lambda *refs: prepare_kernel(experts, *refs),
        out_shape=(matrix_shape, matrix_shape),
        in_specs=[vmem] * 4,
        out_specs=(vmem, vmem),
        compiler_params=limit,
        cost_estimate=cost(4e9, 2e6),
        name="prepare",
    )(fwd_routes, bwd_routes, fwd_weights, bwd_weights)
    total = rows + 2 * group
    worked = pl.pallas_call(
        expert_kernel,
        out_shape=jax.ShapeDtypeStruct((rows, 2 * wide), BF),
        in_specs=[hbm] * 4,
        out_specs=hbm,
        scratch_shapes=[
            pltpu.VMEM((3, total, width), BF),
            pltpu.VMEM((rows, 3 * quarter), BF),
            pltpu.VMEM((local, width, 2 * hidden), BF),
            pltpu.VMEM((local * hidden, width), BF),
            pltpu.VMEM((local, total, 2 * hidden), F32),
            pltpu.VMEM((total, local * hidden), F32),
            pltpu.VMEM((local, bulk + group, hidden), BF),
            pltpu.VMEM((local, bulk + group, 2 * hidden), BF),
            pltpu.VMEM((rows, 2 * quarter), BF),
            pltpu.VMEM((rows, 2 * wide), BF),
            pltpu.SemaphoreType.DMA((4 + 3 * local,)),
            pltpu.SemaphoreType.DMA((2 * ROWS + 1,)),
        ],
        compiler_params=limit,
        cost_estimate=cost(20e9, 22e6),
        name="experts",
    )(arrived, w_gate[0], w_up[0], w_down[0])
    returned = exchange(worked)

    one = jax.ShapeDtypeStruct((tokens, width), BF)
    others = (bwd_matrix, fwd_matrix, bwd_inputs[0], bwd_cotangent[0], fwd_inputs[0], norm_gain)
    section_out, section_grad = pl.pallas_call(
        combine_kernel,
        out_shape=(one, one),
        in_specs=[hbm] * 7,
        out_specs=(vmem, vmem),
        scratch_shapes=[pltpu.VMEM((rows, 2 * wide), BF)]
        + [pltpu.VMEM(other.shape, other.dtype) for other in others]
        + [pltpu.SemaphoreType.DMA((2 * ROWS + 2 + len(others),))],
        compiler_params=limit,
        cost_estimate=cost(4e9, 8e6),
        name="combine",
    )(returned, *others)
    next_forward = from_behind(section_out[None], "segment", 1)
    prev_grad = from_behind(section_grad[None], "segment", -1)
    return (next_forward, prev_grad)


def solution(mesh):
    token = P("segment", ("dp", "expert"), None)
    weight = P("segment", ("dp", "expert"), None, None)
    return jax.shard_map(
        body,
        mesh=mesh,
        in_specs=(token,) * 7 + (P("segment", None),) + (weight,) * 3,
        out_specs=(token, token),
        check_vma=False,
    )
```

```python
import jax
import jax.numpy as jnp
from jax import lax
from jax.experimental import pallas as pl
from jax.experimental.pallas import tpu as pltpu
from jax.sharding import PartitionSpec as P


EPSILON = 1e-06
BF = jnp.bfloat16
F32 = jnp.float32
SLOTS = 5
ROWS = 4
NN = (((1,), (0,)), ((), ()))
NT = (((1,), (1,)), ((), ()))
TN = (((0,), (0,)), ((), ()))


def dot(left, right, dims=NN):
    return lax.dot_general(left, right, dims, preferred_element_type=F32)


def iota(shape, axis):
    return lax.broadcasted_iota(jnp.int32, shape, axis)


def onehot(mask):
    return jnp.where(mask, 1.0, 0.0).astype(BF)


def slot_marks(routes, experts):
    top, tokens = routes.shape
    ids = iota((experts, tokens), 0)
    member = jnp.zeros((experts, tokens), F32)
    for k in range(top):
        member = jnp.where(routes[k : k + 1] == ids, 1.0, member)
    upto = onehot(iota((tokens, tokens), 0) <= iota((tokens, tokens), 1))
    return (dot(member.astype(BF), upto) * member).astype(BF)


def spread_rows(experts):
    rows = experts * ROWS
    return onehot(iota((rows, experts), 0) // ROWS == iota((rows, experts), 1))


def normalize(inputs, norm_scale):
    values = inputs.astype(F32)
    inv_rms = lax.rsqrt(jnp.mean(values * values, axis=-1, keepdims=True) + EPSILON)
    return values * inv_rms * norm_scale, values, inv_rms


def sub(shape):
    return iota(shape, 0) % (2 * ROWS)


def pack_kernel(experts, fwd, bwd, cot, fwd_routes, bwd_routes, gain, out, tile, sems):
    tokens, width = fwd.shape
    quarter = width // ROWS
    rows = experts * ROWS
    copies = []

    def send(at, values):
        cols = pl.ds(at * quarter, quarter)
        tile[:, cols] = values.astype(BF)
        copy = pltpu.make_async_copy(tile.at[:, cols], out.at[:, cols], sems.at[at])
        copy.start()
        copies.append(copy)

    fwd_marks = slot_marks(fwd_routes[...], experts)
    bwd_marks = slot_marks(bwd_routes[...], experts)
    i = iota((rows, experts), 0) // (2 * ROWS)
    e = iota((rows, experts), 1)
    marks = jnp.concatenate([fwd_marks, bwd_marks], axis=1)
    table = [dot(onehot(e == 2 * i + odd), marks) for odd in range(2)]
    pair = (rows, 2 * tokens)
    slot = (sub(pair) % ROWS + 1).astype(F32)
    low = sub(pair) < ROWS
    is_fwd = iota(pair, 1) < tokens
    fwd_rows = normalize(fwd[...], gain[...])[0].astype(BF)
    bwd_rows = normalize(bwd[...], gain[...])[0].astype(BF)
    cot_rows = cot[...]
    both = jnp.concatenate([fwd_rows, bwd_rows], axis=0)
    picks = [
        onehot((table[0] == slot) & (low == is_fwd)),
        onehot((table[1] == slot) & (low != is_fwd)),
    ]
    for block in range(2):
        for q in range(ROWS):
            part = slice(q * quarter, (q + 1) * quarter)
            send(block * ROWS + q, dot(picks[block], both[:, part]))
    crossed = jnp.where(low, table[1], table[0])
    crossed = onehot((crossed == slot) & jnp.logical_not(is_fwd))
    cots = jnp.concatenate([jnp.zeros_like(cot_rows), cot_rows], axis=0)
    for q in range(ROWS):
        part = slice(q * quarter, (q + 1) * quarter)
        send(2 * ROWS + q, dot(crossed, cots[:, part]))
    stacked = [
        jnp.concatenate([v[:, q * quarter : (q + 1) * quarter] for q in range(ROWS)], axis=0)
        for v in (fwd_rows, bwd_rows, cot_rows)
    ]
    spread = spread_rows(experts)
    four = (rows, ROWS * tokens)
    mine = iota(four, 0) % ROWS == iota(four, 1) // tokens
    for a, marks in enumerate((fwd_marks, bwd_marks, bwd_marks)):
        if a < 2:
            wide_table = dot(spread, jnp.concatenate([marks] * ROWS, axis=1))
            last = onehot((wide_table == SLOTS) & mine)
        send(3 * ROWS + a, dot(last, stacked[a]))
    for copy in copies:
        copy.wait()


def weight_matrix(routes, weights, experts):
    top, tokens = routes.shape
    rows = experts * ROWS
    ids = iota((experts, tokens), 0)
    factor = jnp.zeros((experts, tokens), F32)
    for k in range(top):
        factor = jnp.where(routes[k : k + 1] == ids, weights[k : k + 1], factor)
    high = factor.astype(BF)
    low = (factor - high.astype(F32)).astype(BF)
    spread = onehot(iota((experts, rows), 1) // ROWS == iota((experts, rows), 0))
    table = dot(jnp.concatenate([slot_marks(routes, experts), high, low], axis=1), spread, TN)
    slots, halves = table[:tokens], (table[tokens : 2 * tokens], table[2 * tokens :])
    place = iota((tokens, rows), 1) % ROWS
    parts = [jnp.where(slots == (place + 1).astype(F32), half, 0.0) for half in halves]
    for q in range(ROWS):
        parts.extend(jnp.where((slots == SLOTS) & (place == q), half, 0.0) for half in halves)
    return jnp.concatenate([part.astype(BF) for part in parts], axis=0)


def tiles_of(values):
    grouped = values.reshape(values.shape[0] // 16, 2, 8, values.shape[1])
    return grouped[:, 0], grouped[:, 1]


def turn(values):
    return pltpu.roll(values, ROWS, 1)


def is_low(values):
    return iota(values.shape, 1) < ROWS


def half_rows(values, upper):
    even, odd = tiles_of(values)
    if upper:
        joined = jnp.where(is_low(even), turn(even), odd)
    else:
        joined = jnp.where(is_low(even), even, turn(odd))
    return joined.reshape(values.shape[0] // 2, values.shape[1])


def weave(lower, upper):
    shape = (lower.shape[0] // 8, 8, lower.shape[1])
    lower = lower.reshape(shape)
    upper = upper.reshape(shape)
    even = jnp.where(is_low(lower), lower, turn(upper))
    odd = jnp.where(is_low(lower), turn(lower), upper)
    return jnp.stack([even, odd], axis=1).reshape(2 * shape[0] * 8, shape[2])


def expert_kernel(
    arrived, w_gate, w_up, down, out, x, ends, gate_up, gu, h, act, grad, lasts, tile, in_sems,
    out_sems,
):
    local, width, hidden = w_gate.shape
    quarter = width // ROWS
    total = arrived.shape[0]
    groups = total // (local * ROWS)
    bulk = groups * ROWS
    loads = [pltpu.make_async_copy(arrived.at[:, pl.ds(3 * width, 3 * quarter)], ends, in_sems.at[0])]
    for block in range(3):
        loads.append(
            pltpu.make_async_copy(
                arrived.at[:, pl.ds(block * width, width)],
                x.at[block, pl.ds(0, total), :],
                in_sems.at[1 + block],
            )
        )
    for load in loads:
        load.start()
    for i, source in enumerate((w_gate, w_up)):
        loads.append(
            pltpu.make_async_copy(
                source, gate_up.at[:, :, pl.ds(i * hidden, hidden)], in_sems.at[4 + i]
            )
        )
        loads[-1].start()
    c = iota((total, total), 1)
    r = iota((total, total), 0)
    where_from = (r % groups) * (local * ROWS) + r // groups
    loads[0].wait()
    rest = dot(onehot(c == where_from), ends[...]).astype(BF)
    for a, e, block, place in (
        (0, 0, 0, 0), (1, 0, 0, 1), (1, 1, 1, 0), (0, 1, 1, 1), (2, 1, 2, 0), (2, 0, 2, 1),
    ):
        for q in range(ROWS):
            at = (e * ROWS + q) * groups
            x[block, pl.ds(total + place * groups, groups), pl.ds(q * quarter, quarter)] = rest[
                at : at + groups, a * quarter : (a + 1) * quarter
            ]

    step = 2 * hidden // 3
    third = hidden // 3

    def gate_up_of(e):
        for n in range(3):
            cols = pl.ds(n * step, step)
            gu[e, :, cols] = dot(x[e], gate_up[e, :, cols])

    def take(values, e, forward):
        upper = forward == (e == 1)
        main = half_rows(values[:total], upper)
        at = total + groups * int(upper)
        return jnp.concatenate([main, values[at : at + groups]], axis=0)

    def forward_of(e):
        for at in range(0, hidden, third):
            g = take(gu[e, :, pl.ds(at, third)], e, True)
            u = take(gu[e, :, pl.ds(hidden + at, third)], e, True)
            act[e, :, pl.ds(at, third)] = (g * jax.nn.sigmoid(g) * u).astype(BF)

    def backward_of(e):
        for at in range(0, hidden, third):
            g = take(gu[e, :, pl.ds(at, third)], e, False)
            u = take(gu[e, :, pl.ds(hidden + at, third)], e, False)
            b = take(h[:, pl.ds(e * hidden + at, third)], e, False)
            s = jax.nn.sigmoid(g)
            grad[e, :, pl.ds(at, third)] = (b * u * s * (1.0 + g * (1.0 - s))).astype(BF)
            grad[e, :, pl.ds(hidden + at, third)] = (b * g * s).astype(BF)

    copies = []
    back_to = onehot(r == (c % groups) * (local * ROWS) + c // groups)

    def ship(at):
        cols = pl.ds(at * quarter, quarter)
        copy = pltpu.make_async_copy(tile.at[:, cols], out.at[:, cols], out_sems.at[at])
        copy.start()
        copies.append(copy)

    def send_back(a, q):
        part = pl.ds(q * quarter, quarter)
        if a == 0:
            o = [dot(act[e], down[pl.ds(e * hidden, hidden), part]) for e in range(local)]
        else:
            o = [dot(grad[e], gate_up[e, part, :], NT) for e in range(local)]
        tile[:, pl.ds((a * ROWS + q) * quarter, quarter)] = weave(o[0][:bulk], o[1][:bulk]).astype(BF)
        for e in range(local):
            lasts[pl.ds((e * ROWS + q) * groups, groups), pl.ds(a * quarter, quarter)] = o[e][
                bulk:
            ].astype(BF)
        ship(a * ROWS + q)

    def send_back_last(a):
        tile[:, pl.ds((2 * ROWS + a) * quarter, quarter)] = dot(
            back_to, lasts[:, pl.ds(a * quarter, quarter)]
        ).astype(BF)
        ship(2 * ROWS + a)

    for load in loads[1:3] + loads[4:]:
        load.wait()
    gate_up_of(0)
    gate_up_of(1)
    forward_of(0)
    loads[3].wait()
    for n in range(3):
        cols = pl.ds(n * step, step)
        h[:, cols] = dot(x[2], down[cols, :], NT)
    forward_of(1)
    for q in range(ROWS):
        send_back(0, q)
    backward_of(0)
    backward_of(1)
    send_back_last(0)
    for q in range(ROWS):
        send_back(1, q)
    send_back_last(1)
    for copy in copies:
        copy.wait()


def weighted_sum(part, returned, matrix):
    tokens = matrix.shape[0] // (2 + 2 * ROWS)
    quarter = returned.shape[1] // (2 * ROWS + 2)
    pieces = []
    for q in range(ROWS):
        at = part * ROWS + q
        piece = dot(matrix[: 2 * tokens], returned[:, pl.ds(at * quarter, quarter)])
        pieces.append(piece[:tokens] + piece[tokens:])
    at = 2 * ROWS + part
    extra = dot(matrix[2 * tokens :], returned[:, pl.ds(at * quarter, quarter)])
    for q in range(ROWS):
        at = 2 * q * tokens
        pieces[q] += extra[at : at + tokens] + extra[at + tokens : at + 2 * tokens]
    return jnp.concatenate(pieces, axis=1)


def combine_kernel(
    experts, returned, fwd_routes, bwd_routes, fwd_weights, bwd_weights, bwd_inputs, cot,
    fwd_inputs, gain, fwd_out, bwd_out,
):
    fwd_matrix = weight_matrix(fwd_routes[...], fwd_weights[...], experts)
    combined = weighted_sum(0, returned, fwd_matrix)
    fwd_out[...] = (fwd_inputs[...].astype(F32) + combined).astype(BF)
    bwd_matrix = weight_matrix(bwd_routes[...], bwd_weights[...], experts)
    norm_grad = weighted_sum(1, returned, bwd_matrix)
    norm_scale = gain[...]
    _, values, inv_rms = normalize(bwd_inputs[...], norm_scale)
    scaled = norm_scale * norm_grad
    mean = jnp.mean(values * scaled, axis=-1, keepdims=True)
    bwd_out[...] = (
        cot[...].astype(F32) + inv_rms * scaled - values * (inv_rms * inv_rms * inv_rms) * mean
    ).astype(BF)


def from_behind(value, axis, steps):
    count = lax.axis_size(axis)
    pairs = [(source, (source + steps) % count) for source in range(count)]
    return lax.ppermute(value, axis, pairs)


def body(
    fwd_inputs,
    fwd_routes,
    fwd_weights,
    bwd_inputs,
    bwd_cotangent,
    bwd_routes,
    bwd_weights,
    norm_gain,
    w_gate,
    w_up,
    w_down,
):
    _, tokens, width = fwd_inputs.shape
    local = w_gate.shape[1]
    hidden = w_gate.shape[3]
    group = lax.axis_size("dp") * lax.axis_size("expert")
    experts = local * group
    rows = experts * ROWS
    quarter = width // ROWS
    wide = width + quarter
    bulk = group * ROWS
    vmem = pl.BlockSpec(memory_space=pltpu.VMEM)
    hbm = pl.BlockSpec(memory_space=pltpu.HBM)
    limit = pltpu.CompilerParams(vmem_limit_bytes=65_000_000)
    fwd_routes = fwd_routes[0].T
    bwd_routes = bwd_routes[0].T
    fwd_weights = fwd_weights[0].T
    bwd_weights = bwd_weights[0].T

    def cost(flops, moved):
        return pl.CostEstimate(flops=int(flops), bytes_accessed=int(moved), transcendentals=0)

    def exchange(packed):
        return lax.all_to_all(packed, ("dp", "expert"), split_axis=0, concat_axis=0, tiled=True)

    packed = pl.pallas_call(
        lambda *refs: pack_kernel(experts, *refs),
        out_shape=jax.ShapeDtypeStruct((rows, 3 * wide), BF),
        in_specs=[vmem] * 6,
        out_specs=hbm,
        scratch_shapes=[
            pltpu.VMEM((rows, 3 * wide), BF),
            pltpu.SemaphoreType.DMA((3 * (ROWS + 1),)),
        ],
        compiler_params=limit,
        cost_estimate=cost(9e9, 9e6),
        name="pack",
    )(fwd_inputs[0], bwd_inputs[0], bwd_cotangent[0], fwd_routes, bwd_routes, norm_gain)
    arrived = exchange(packed)
    total = rows + 2 * group
    worked = pl.pallas_call(
        expert_kernel,
        out_shape=jax.ShapeDtypeStruct((rows, 2 * wide), BF),
        in_specs=[hbm] + [vmem] * 3,
        out_specs=hbm,
        scratch_shapes=[
            pltpu.VMEM((3, total, width), BF),
            pltpu.VMEM((rows, 3 * quarter), BF),
            pltpu.VMEM((local, width, 2 * hidden), BF),
            pltpu.VMEM((local, total, 2 * hidden), F32),
            pltpu.VMEM((total, local * hidden), F32),
            pltpu.VMEM((local, bulk + group, hidden), BF),
            pltpu.VMEM((local, bulk + group, 2 * hidden), BF),
            pltpu.VMEM((rows, 2 * quarter), BF),
            pltpu.VMEM((rows, 2 * wide), BF),
            pltpu.SemaphoreType.DMA((6,)),
            pltpu.SemaphoreType.DMA((2 * ROWS + 2,)),
        ],
        compiler_params=pltpu.CompilerParams(vmem_limit_bytes=40 * 1024 * 1024),
        cost_estimate=cost(20e9, 22e6),
        name="experts",
    )(
        arrived,
        w_gate[0],
        w_up[0],
        w_down[0].reshape(local * hidden, width),
    )
    returned = exchange(worked)

    one = jax.ShapeDtypeStruct((tokens, width), BF)
    section_out, section_grad = pl.pallas_call(
        lambda *refs: combine_kernel(experts, *refs),
        out_shape=(one, one),
        in_specs=[vmem] * 9,
        out_specs=(vmem, vmem),
        compiler_params=pltpu.CompilerParams(vmem_limit_bytes=16 * 1024 * 1024),
        cost_estimate=cost(4e9, 8e6),
        name="combine",
    )(
        returned,
        fwd_routes,
        bwd_routes,
        fwd_weights,
        bwd_weights,
        bwd_inputs[0],
        bwd_cotangent[0],
        fwd_inputs[0],
        norm_gain,
    )
    next_forward = from_behind(section_out[None], "segment", 1)
    prev_grad = from_behind(section_grad[None], "segment", -1)
    return (next_forward, prev_grad)


def solution(mesh):
    token = P("segment", ("dp", "expert"), None)
    weight = P("segment", ("dp", "expert"), None, None)
    return jax.shard_map(
        body,
        mesh=mesh,
        in_specs=(token,) * 7 + (P("segment", None),) + (weight,) * 3,
        out_specs=(token, token),
        check_vma=False,
    )
```

```python
import jax
import jax.numpy as jnp
from jax import lax
from jax.experimental import pallas as pl
from jax.experimental.pallas import tpu as pltpu
from jax.sharding import PartitionSpec as P


EPSILON = 1e-06
BF = jnp.bfloat16
F32 = jnp.float32
SLOTS = 5
ROWS = 4
NN = (((1,), (0,)), ((), ()))
NT = (((1,), (1,)), ((), ()))
TN = (((0,), (0,)), ((), ()))


def dot(left, right, dims=NN):
    return lax.dot_general(left, right, dims, preferred_element_type=F32)


def iota(shape, axis):
    return lax.broadcasted_iota(jnp.int32, shape, axis)


def onehot(mask):
    return jnp.where(mask, 1.0, 0.0).astype(BF)


def slot_marks(routes, experts):
    top, tokens = routes.shape
    ids = iota((experts, tokens), 0)
    member = jnp.zeros((experts, tokens), F32)
    for k in range(top):
        member = jnp.where(routes[k : k + 1] == ids, 1.0, member)
    upto = onehot(iota((tokens, tokens), 0) <= iota((tokens, tokens), 1))
    return (dot(member.astype(BF), upto) * member).astype(BF)


def spread_rows(experts):
    rows = experts * ROWS
    return onehot(iota((rows, experts), 0) // ROWS == iota((rows, experts), 1))


def normalize(inputs, norm_scale):
    values = inputs.astype(F32)
    inv_rms = lax.rsqrt(jnp.mean(values * values, axis=-1, keepdims=True) + EPSILON)
    return values * inv_rms * norm_scale, values, inv_rms


def sub(shape):
    return iota(shape, 0) % (2 * ROWS)


def pack_kernel(experts, fwd, bwd, cot, fwd_routes, bwd_routes, gain, out, tile, sems):
    tokens, width = fwd.shape
    quarter = width // ROWS
    rows = experts * ROWS
    copies = []

    def send(at, values):
        cols = pl.ds(at * quarter, quarter)
        tile[:, cols] = values.astype(BF)
        copy = pltpu.make_async_copy(tile.at[:, cols], out.at[:, cols], sems.at[at])
        copy.start()
        copies.append(copy)

    fwd_marks = slot_marks(fwd_routes[...], experts)
    bwd_marks = slot_marks(bwd_routes[...], experts)
    i = iota((rows, experts), 0) // (2 * ROWS)
    e = iota((rows, experts), 1)
    marks = jnp.concatenate([fwd_marks, bwd_marks], axis=1)
    table = [dot(onehot(e == 2 * i + odd), marks) for odd in range(2)]
    pair = (rows, 2 * tokens)
    slot = (sub(pair) % ROWS + 1).astype(F32)
    low = sub(pair) < ROWS
    is_fwd = iota(pair, 1) < tokens
    fwd_rows = normalize(fwd[...], gain[...])[0].astype(BF)
    bwd_rows = normalize(bwd[...], gain[...])[0].astype(BF)
    cot_rows = cot[...]
    both = jnp.concatenate([fwd_rows, bwd_rows], axis=0)
    picks = [
        onehot((table[0] == slot) & (low == is_fwd)),
        onehot((table[1] == slot) & (low != is_fwd)),
    ]
    for block in range(2):
        for q in range(ROWS):
            part = slice(q * quarter, (q + 1) * quarter)
            send(block * ROWS + q, dot(picks[block], both[:, part]))
    crossed = jnp.where(low, table[1], table[0])
    crossed = onehot((crossed == slot) & jnp.logical_not(is_fwd))
    cots = jnp.concatenate([jnp.zeros_like(cot_rows), cot_rows], axis=0)
    for q in range(ROWS):
        part = slice(q * quarter, (q + 1) * quarter)
        send(2 * ROWS + q, dot(crossed, cots[:, part]))
    stacked = [
        jnp.concatenate([v[:, q * quarter : (q + 1) * quarter] for q in range(ROWS)], axis=0)
        for v in (fwd_rows, bwd_rows, cot_rows)
    ]
    spread = spread_rows(experts)
    four = (rows, ROWS * tokens)
    mine = iota(four, 0) % ROWS == iota(four, 1) // tokens
    for a, marks in enumerate((fwd_marks, bwd_marks, bwd_marks)):
        if a < 2:
            wide_table = dot(spread, jnp.concatenate([marks] * ROWS, axis=1))
            last = onehot((wide_table == SLOTS) & mine)
        send(3 * ROWS + a, dot(last, stacked[a]))
    for copy in copies:
        copy.wait()


def weight_matrix(routes, weights, experts):
    top, tokens = routes.shape
    rows = experts * ROWS
    ids = iota((experts, tokens), 0)
    factor = jnp.zeros((experts, tokens), F32)
    for k in range(top):
        factor = jnp.where(routes[k : k + 1] == ids, weights[k : k + 1], factor)
    high = factor.astype(BF)
    low = (factor - high.astype(F32)).astype(BF)
    spread = onehot(iota((experts, rows), 1) // ROWS == iota((experts, rows), 0))
    table = dot(jnp.concatenate([slot_marks(routes, experts), high, low], axis=1), spread, TN)
    slots, halves = table[:tokens], (table[tokens : 2 * tokens], table[2 * tokens :])
    place = iota((tokens, rows), 1) % ROWS
    parts = [jnp.where(slots == (place + 1).astype(F32), half, 0.0) for half in halves]
    for q in range(ROWS):
        parts.extend(jnp.where((slots == SLOTS) & (place == q), half, 0.0) for half in halves)
    return jnp.concatenate([part.astype(BF) for part in parts], axis=0)


def tiles_of(values):
    grouped = values.reshape(values.shape[0] // 16, 2, 8, values.shape[1])
    return grouped[:, 0], grouped[:, 1]


def turn(values):
    return pltpu.roll(values, ROWS, 1)


def is_low(values):
    return iota(values.shape, 1) < ROWS


def half_rows(values, upper):
    even, odd = tiles_of(values)
    if upper:
        joined = jnp.where(is_low(even), turn(even), odd)
    else:
        joined = jnp.where(is_low(even), even, turn(odd))
    return joined.reshape(values.shape[0] // 2, values.shape[1])


def weave(lower, upper):
    shape = (lower.shape[0] // 8, 8, lower.shape[1])
    lower = lower.reshape(shape)
    upper = upper.reshape(shape)
    even = jnp.where(is_low(lower), lower, turn(upper))
    odd = jnp.where(is_low(lower), turn(lower), upper)
    return jnp.stack([even, odd], axis=1).reshape(2 * shape[0] * 8, shape[2])


def expert_kernel(
    arrived, w_gate, w_up, down, tile, x, gate_up, gu, h, act, grad, lasts, in_sems
):
    local, width, hidden = w_gate.shape
    quarter = width // ROWS
    total = arrived.shape[0]
    groups = total // (local * ROWS)
    bulk = groups * ROWS
    joins = []
    for i, source in enumerate((w_gate, w_up)):
        joins.append(
            pltpu.make_async_copy(
                source, gate_up.at[:, :, pl.ds(i * hidden, hidden)], in_sems.at[i]
            )
        )
        joins[i].start()

    c = iota((total, total), 1)
    r = iota((total, total), 0)
    where_from = (r % groups) * (local * ROWS) + r // groups
    rest = dot(onehot(c == where_from), arrived[:, pl.ds(3 * width, 3 * quarter)]).astype(BF)
    for a, e, block, place in (
        (2, 1, 2, 0), (2, 0, 2, 1), (0, 0, 0, 0), (1, 0, 0, 1), (1, 1, 1, 0), (0, 1, 1, 1),
    ):
        for q in range(ROWS):
            at = (e * ROWS + q) * groups
            x[block, pl.ds(place * groups, groups), pl.ds(q * quarter, quarter)] = rest[
                at : at + groups, a * quarter : (a + 1) * quarter
            ]

    def rows_of(block):
        return jnp.concatenate([arrived[:, pl.ds(block * width, width)], x[block]], axis=0)

    step = 2 * hidden // 3
    third = hidden // 3

    def gate_up_of(e):
        for n in range(3):
            cols = pl.ds(n * step, step)
            gu[e, :, cols] = dot(rows_of(e), gate_up[e, :, cols])

    def take(values, e, forward):
        upper = forward == (e == 1)
        main = half_rows(values[:total], upper)
        at = total + groups * int(upper)
        return jnp.concatenate([main, values[at : at + groups]], axis=0)

    def forward_of(e):
        for at in range(0, hidden, third):
            g = take(gu[e, :, pl.ds(at, third)], e, True)
            u = take(gu[e, :, pl.ds(hidden + at, third)], e, True)
            act[e, :, pl.ds(at, third)] = (g * jax.nn.sigmoid(g) * u).astype(BF)

    def backward_of(e):
        for at in range(0, hidden, third):
            g = take(gu[e, :, pl.ds(at, third)], e, False)
            u = take(gu[e, :, pl.ds(hidden + at, third)], e, False)
            b = take(h[:, pl.ds(e * hidden + at, third)], e, False)
            s = jax.nn.sigmoid(g)
            grad[e, :, pl.ds(at, third)] = (b * u * s * (1.0 + g * (1.0 - s))).astype(BF)
            grad[e, :, pl.ds(hidden + at, third)] = (b * g * s).astype(BF)

    back_to = onehot(r == (c % groups) * (local * ROWS) + c // groups)

    def send_back(a, q):
        part = pl.ds(q * quarter, quarter)
        if a == 0:
            o = [dot(act[e], down[pl.ds(e * hidden, hidden), part]) for e in range(local)]
        else:
            o = [dot(grad[e], gate_up[e, part, :], NT) for e in range(local)]
        tile[:, pl.ds((a * ROWS + q) * quarter, quarter)] = weave(o[0][:bulk], o[1][:bulk]).astype(BF)
        for e in range(local):
            lasts[pl.ds((e * ROWS + q) * groups, groups), pl.ds(a * quarter, quarter)] = o[e][
                bulk:
            ].astype(BF)

    def send_back_last(a):
        tile[:, pl.ds((2 * ROWS + a) * quarter, quarter)] = dot(
            back_to, lasts[:, pl.ds(a * quarter, quarter)]
        ).astype(BF)

    for n in range(3):
        cols = pl.ds(n * step, step)
        h[:, cols] = dot(rows_of(2), down[cols, :], NT)
    for join in joins:
        join.wait()
    gate_up_of(0)
    gate_up_of(1)
    forward_of(0)
    forward_of(1)
    for q in range(ROWS):
        send_back(0, q)
    backward_of(0)
    backward_of(1)
    send_back_last(0)
    for q in range(ROWS):
        send_back(1, q)
    send_back_last(1)


def weighted_sum(part, returned, matrix):
    tokens = matrix.shape[0] // (2 + 2 * ROWS)
    quarter = returned.shape[1] // (2 * ROWS + 2)
    pieces = []
    for q in range(ROWS):
        at = part * ROWS + q
        piece = dot(matrix[: 2 * tokens], returned[:, pl.ds(at * quarter, quarter)])
        pieces.append(piece[:tokens] + piece[tokens:])
    at = 2 * ROWS + part
    extra = dot(matrix[2 * tokens :], returned[:, pl.ds(at * quarter, quarter)])
    for q in range(ROWS):
        at = 2 * q * tokens
        pieces[q] += extra[at : at + tokens] + extra[at + tokens : at + 2 * tokens]
    return jnp.concatenate(pieces, axis=1)


def combine_kernel(
    experts, returned, fwd_routes, bwd_routes, fwd_weights, bwd_weights, bwd_inputs, cot,
    fwd_inputs, gain, fwd_out, bwd_out,
):
    fwd_matrix = weight_matrix(fwd_routes[...], fwd_weights[...], experts)
    combined = weighted_sum(0, returned, fwd_matrix)
    fwd_out[...] = (fwd_inputs[...].astype(F32) + combined).astype(BF)
    bwd_matrix = weight_matrix(bwd_routes[...], bwd_weights[...], experts)
    norm_grad = weighted_sum(1, returned, bwd_matrix)
    norm_scale = gain[...]
    _, values, inv_rms = normalize(bwd_inputs[...], norm_scale)
    scaled = norm_scale * norm_grad
    mean = jnp.mean(values * scaled, axis=-1, keepdims=True)
    bwd_out[...] = (
        cot[...].astype(F32) + inv_rms * scaled - values * (inv_rms * inv_rms * inv_rms) * mean
    ).astype(BF)


def from_behind(value, axis, steps):
    count = lax.axis_size(axis)
    pairs = [(source, (source + steps) % count) for source in range(count)]
    return lax.ppermute(value, axis, pairs)


def body(
    fwd_inputs,
    fwd_routes,
    fwd_weights,
    bwd_inputs,
    bwd_cotangent,
    bwd_routes,
    bwd_weights,
    norm_gain,
    w_gate,
    w_up,
    w_down,
):
    _, tokens, width = fwd_inputs.shape
    local = w_gate.shape[1]
    hidden = w_gate.shape[3]
    group = lax.axis_size("dp") * lax.axis_size("expert")
    experts = local * group
    rows = experts * ROWS
    quarter = width // ROWS
    wide = width + quarter
    bulk = group * ROWS
    vmem = pl.BlockSpec(memory_space=pltpu.VMEM)
    hbm = pl.BlockSpec(memory_space=pltpu.HBM)
    limit = pltpu.CompilerParams(vmem_limit_bytes=65_000_000)
    fwd_routes = fwd_routes[0].T
    bwd_routes = bwd_routes[0].T
    fwd_weights = fwd_weights[0].T
    bwd_weights = bwd_weights[0].T

    def cost(flops, moved):
        return pl.CostEstimate(flops=int(flops), bytes_accessed=int(moved), transcendentals=0)

    def exchange(packed):
        return lax.all_to_all(packed, ("dp", "expert"), split_axis=0, concat_axis=0, tiled=True)

    packed = pl.pallas_call(
        lambda *refs: pack_kernel(experts, *refs),
        out_shape=jax.ShapeDtypeStruct((rows, 3 * wide), BF),
        in_specs=[vmem] * 6,
        out_specs=hbm,
        scratch_shapes=[
            pltpu.VMEM((rows, 3 * wide), BF),
            pltpu.SemaphoreType.DMA((3 * (ROWS + 1),)),
        ],
        compiler_params=limit,
        cost_estimate=cost(9e9, 9e6),
        name="pack",
    )(fwd_inputs[0], bwd_inputs[0], bwd_cotangent[0], fwd_routes, bwd_routes, norm_gain)
    arrived = exchange(packed)
    total = rows + 2 * group
    worked = pl.pallas_call(
        expert_kernel,
        out_shape=jax.ShapeDtypeStruct((rows, 2 * wide), BF),
        in_specs=[vmem] * 4,
        out_specs=vmem,
        scratch_shapes=[
            pltpu.VMEM((3, 2 * group, width), BF),
            pltpu.VMEM((local, width, 2 * hidden), BF),
            pltpu.VMEM((local, total, 2 * hidden), F32),
            pltpu.VMEM((total, local * hidden), F32),
            pltpu.VMEM((local, bulk + group, hidden), BF),
            pltpu.VMEM((local, bulk + group, 2 * hidden), BF),
            pltpu.VMEM((rows, 2 * quarter), BF),
            pltpu.SemaphoreType.DMA((2,)),
        ],
        compiler_params=pltpu.CompilerParams(vmem_limit_bytes=28 * 1024 * 1024),
        cost_estimate=cost(20e9, 22e6),
        name="experts",
    )(
        arrived,
        w_gate[0],
        w_up[0],
        w_down[0].reshape(local * hidden, width),
    )
    returned = exchange(worked)

    one = jax.ShapeDtypeStruct((tokens, width), BF)
    section_out, section_grad = pl.pallas_call(
        lambda *refs: combine_kernel(experts, *refs),
        out_shape=(one, one),
        in_specs=[vmem] * 9,
        out_specs=(vmem, vmem),
        compiler_params=pltpu.CompilerParams(vmem_limit_bytes=16 * 1024 * 1024),
        cost_estimate=cost(4e9, 8e6),
        name="combine",
    )(
        returned,
        fwd_routes,
        bwd_routes,
        fwd_weights,
        bwd_weights,
        bwd_inputs[0],
        bwd_cotangent[0],
        fwd_inputs[0],
        norm_gain,
    )
    next_forward = from_behind(section_out[None], "segment", 1)
    prev_grad = from_behind(section_grad[None], "segment", -1)
    return (next_forward, prev_grad)


def solution(mesh):
    token = P("segment", ("dp", "expert"), None)
    weight = P("segment", ("dp", "expert"), None, None)
    return jax.shard_map(
        body,
        mesh=mesh,
        in_specs=(token,) * 7 + (P("segment", None),) + (weight,) * 3,
        out_specs=(token, token),
        check_vma=False,
    )
```

```python
import jax
import jax.numpy as jnp
from jax import lax
from jax.experimental import pallas as pl
from jax.experimental.pallas import tpu as pltpu
from jax.sharding import PartitionSpec as P


EPSILON = 1e-06
BF = jnp.bfloat16
F32 = jnp.float32
SLOTS = 5
ROWS = 4
LOCAL = 2
NN = (((1,), (0,)), ((), ()))
NT = (((1,), (1,)), ((), ()))
TN = (((0,), (0,)), ((), ()))


def dot(left, right, dims=NN):
    return lax.dot_general(left, right, dims, preferred_element_type=F32)


def iota(shape, axis):
    return lax.broadcasted_iota(jnp.int32, shape, axis)


def onehot(mask):
    return jnp.where(mask, 1.0, 0.0).astype(BF)


def wire_ids(experts, tokens):
    at = iota((experts, tokens), 0)
    count = lax.axis_size("dp")
    device = (at // LOCAL) % count * (experts // LOCAL // count) + at // LOCAL // count
    return device * LOCAL + at % LOCAL


def slot_marks(routes, experts):
    top, tokens = routes.shape
    ids = wire_ids(experts, tokens)
    member = jnp.zeros((experts, tokens), F32)
    for k in range(top):
        member = jnp.where(routes[k : k + 1] == ids, 1.0, member)
    upto = onehot(iota((tokens, tokens), 0) <= iota((tokens, tokens), 1))
    return (dot(member.astype(BF), upto) * member).astype(BF)


def spread_rows(experts):
    rows = experts * ROWS
    return onehot(iota((rows, experts), 0) // ROWS == iota((rows, experts), 1))


def normalize(inputs, norm_scale):
    values = inputs.astype(F32)
    inv_rms = lax.rsqrt(jnp.mean(values * values, axis=-1, keepdims=True) + EPSILON)
    return values * inv_rms * norm_scale, values, inv_rms


def sub(shape):
    return iota(shape, 0) % (2 * ROWS)


def pack_kernel(experts, fwd, bwd, cot, fwd_routes, bwd_routes, gain, out, tile, sems):
    tokens, width = fwd.shape
    quarter = width // ROWS
    rows = experts * ROWS
    copies = []

    def send(at, values):
        cols = pl.ds(at * quarter, quarter)
        tile[:, cols] = values.astype(BF)
        copy = pltpu.make_async_copy(tile.at[:, cols], out.at[:, cols], sems.at[at])
        copy.start()
        copies.append(copy)

    fwd_marks = slot_marks(fwd_routes[...], experts)
    bwd_marks = slot_marks(bwd_routes[...], experts)
    i = iota((rows, experts), 0) // (2 * ROWS)
    e = iota((rows, experts), 1)
    marks = jnp.concatenate([fwd_marks, bwd_marks], axis=1)
    table = [dot(onehot(e == 2 * i + odd), marks) for odd in range(2)]
    pair = (rows, 2 * tokens)
    slot = (sub(pair) % ROWS + 1).astype(F32)
    low = sub(pair) < ROWS
    is_fwd = iota(pair, 1) < tokens
    fwd_rows = normalize(fwd[...], gain[...])[0].astype(BF)
    bwd_rows = normalize(bwd[...], gain[...])[0].astype(BF)
    cot_rows = cot[...]
    both = jnp.concatenate([fwd_rows, bwd_rows], axis=0)
    picks = [
        onehot((table[0] == slot) & (low == is_fwd)),
        onehot((table[1] == slot) & (low != is_fwd)),
    ]
    for block in range(2):
        for q in range(ROWS):
            part = slice(q * quarter, (q + 1) * quarter)
            send(block * ROWS + q, dot(picks[block], both[:, part]))
    crossed = jnp.where(low, table[1], table[0])
    crossed = onehot((crossed == slot) & jnp.logical_not(is_fwd))
    cots = jnp.concatenate([jnp.zeros_like(cot_rows), cot_rows], axis=0)
    for q in range(ROWS):
        part = slice(q * quarter, (q + 1) * quarter)
        send(2 * ROWS + q, dot(crossed, cots[:, part]))
    stacked = [
        jnp.concatenate([v[:, q * quarter : (q + 1) * quarter] for q in range(ROWS)], axis=0)
        for v in (fwd_rows, bwd_rows, cot_rows)
    ]
    spread = spread_rows(experts)
    four = (rows, ROWS * tokens)
    mine = iota(four, 0) % ROWS == iota(four, 1) // tokens
    for a, marks in enumerate((fwd_marks, bwd_marks, bwd_marks)):
        if a < 2:
            wide_table = dot(spread, jnp.concatenate([marks] * ROWS, axis=1))
            last = onehot((wide_table == SLOTS) & mine)
        send(3 * ROWS + a, dot(last, stacked[a]))
    for copy in copies:
        copy.wait()


def weight_matrix(routes, weights, experts):
    top, tokens = routes.shape
    rows = experts * ROWS
    ids = wire_ids(experts, tokens)
    factor = jnp.zeros((experts, tokens), F32)
    for k in range(top):
        factor = jnp.where(routes[k : k + 1] == ids, weights[k : k + 1], factor)
    high = factor.astype(BF)
    low = (factor - high.astype(F32)).astype(BF)
    spread = onehot(iota((experts, rows), 1) // ROWS == iota((experts, rows), 0))
    table = dot(jnp.concatenate([slot_marks(routes, experts), high, low], axis=1), spread, TN)
    slots, halves = table[:tokens], (table[tokens : 2 * tokens], table[2 * tokens :])
    place = iota((tokens, rows), 1) % ROWS
    parts = [jnp.where(slots == (place + 1).astype(F32), half, 0.0) for half in halves]
    for q in range(ROWS):
        parts.extend(jnp.where((slots == SLOTS) & (place == q), half, 0.0) for half in halves)
    return jnp.concatenate([part.astype(BF) for part in parts], axis=0)


def tiles_of(values):
    grouped = values.reshape(values.shape[0] // 16, 2, 8, values.shape[1])
    return grouped[:, 0], grouped[:, 1]


def turn(values):
    return pltpu.roll(values, ROWS, 1)


def is_low(values):
    return iota(values.shape, 1) < ROWS


def half_rows(values, upper):
    even, odd = tiles_of(values)
    if upper:
        joined = jnp.where(is_low(even), turn(even), odd)
    else:
        joined = jnp.where(is_low(even), even, turn(odd))
    return joined.reshape(values.shape[0] // 2, values.shape[1])


def weave(lower, upper):
    shape = (lower.shape[0] // 8, 8, lower.shape[1])
    lower = lower.reshape(shape)
    upper = upper.reshape(shape)
    even = jnp.where(is_low(lower), lower, turn(upper))
    odd = jnp.where(is_low(lower), turn(lower), upper)
    return jnp.stack([even, odd], axis=1).reshape(2 * shape[0] * 8, shape[2])


def expert_kernel(
    arrived, w_gate, w_up, down, tile, x, gate_up, gu, h, act, grad, lasts, in_sems
):
    local, width, hidden = w_gate.shape
    quarter = width // ROWS
    total = arrived.shape[0]
    groups = total // (local * ROWS)
    bulk = groups * ROWS
    joins = []
    for i, source in enumerate((w_gate, w_up)):
        joins.append(
            pltpu.make_async_copy(
                source, gate_up.at[:, :, pl.ds(i * hidden, hidden)], in_sems.at[i]
            )
        )
        joins[i].start()

    c = iota((total, total), 1)
    r = iota((total, total), 0)
    where_from = (r % groups) * (local * ROWS) + r // groups
    rest = dot(onehot(c == where_from), arrived[:, pl.ds(3 * width, 3 * quarter)]).astype(BF)
    for a, e, block, place in (
        (2, 1, 2, 0), (2, 0, 2, 1), (0, 0, 0, 0), (1, 0, 0, 1), (1, 1, 1, 0), (0, 1, 1, 1),
    ):
        for q in range(ROWS):
            at = (e * ROWS + q) * groups
            x[block, pl.ds(place * groups, groups), pl.ds(q * quarter, quarter)] = rest[
                at : at + groups, a * quarter : (a + 1) * quarter
            ]

    def rows_of(block):
        return jnp.concatenate([arrived[:, pl.ds(block * width, width)], x[block]], axis=0)

    step = 2 * hidden // 3
    third = hidden // 3

    def gate_up_of(e):
        for n in range(3):
            cols = pl.ds(n * step, step)
            gu[e, :, cols] = dot(rows_of(e), gate_up[e, :, cols])

    def take(values, e, forward):
        upper = forward == (e == 1)
        main = half_rows(values[:total], upper)
        at = total + groups * int(upper)
        return jnp.concatenate([main, values[at : at + groups]], axis=0)

    def forward_of(e):
        for at in range(0, hidden, third):
            g = take(gu[e, :, pl.ds(at, third)], e, True)
            u = take(gu[e, :, pl.ds(hidden + at, third)], e, True)
            act[e, :, pl.ds(at, third)] = (g * jax.nn.sigmoid(g) * u).astype(BF)

    def backward_of(e):
        for at in range(0, hidden, third):
            g = take(gu[e, :, pl.ds(at, third)], e, False)
            u = take(gu[e, :, pl.ds(hidden + at, third)], e, False)
            b = take(h[:, pl.ds(e * hidden + at, third)], e, False)
            s = jax.nn.sigmoid(g)
            grad[e, :, pl.ds(at, third)] = (b * u * s * (1.0 + g * (1.0 - s))).astype(BF)
            grad[e, :, pl.ds(hidden + at, third)] = (b * g * s).astype(BF)

    back_to = onehot(r == (c % groups) * (local * ROWS) + c // groups)

    def send_back(a, q):
        part = pl.ds(q * quarter, quarter)
        if a == 0:
            o = [dot(act[e], down[pl.ds(e * hidden, hidden), part]) for e in range(local)]
        else:
            o = [dot(grad[e], gate_up[e, part, :], NT) for e in range(local)]
        tile[:, pl.ds((a * ROWS + q) * quarter, quarter)] = weave(o[0][:bulk], o[1][:bulk]).astype(BF)
        for e in range(local):
            lasts[pl.ds((e * ROWS + q) * groups, groups), pl.ds(a * quarter, quarter)] = o[e][
                bulk:
            ].astype(BF)

    def send_back_last(a):
        tile[:, pl.ds((2 * ROWS + a) * quarter, quarter)] = dot(
            back_to, lasts[:, pl.ds(a * quarter, quarter)]
        ).astype(BF)

    for n in range(3):
        cols = pl.ds(n * step, step)
        h[:, cols] = dot(rows_of(2), down[cols, :], NT)
    for join in joins:
        join.wait()
    gate_up_of(0)
    gate_up_of(1)
    forward_of(0)
    forward_of(1)
    for q in range(ROWS):
        send_back(0, q)
    backward_of(0)
    backward_of(1)
    send_back_last(0)
    for q in range(ROWS):
        send_back(1, q)
    send_back_last(1)


def weighted_sum(part, returned, matrix):
    tokens = matrix.shape[0] // (2 + 2 * ROWS)
    quarter = returned.shape[1] // (2 * ROWS + 2)
    pieces = []
    for q in range(ROWS):
        at = part * ROWS + q
        piece = dot(matrix[: 2 * tokens], returned[:, pl.ds(at * quarter, quarter)])
        pieces.append(piece[:tokens] + piece[tokens:])
    at = 2 * ROWS + part
    extra = dot(matrix[2 * tokens :], returned[:, pl.ds(at * quarter, quarter)])
    for q in range(ROWS):
        at = 2 * q * tokens
        pieces[q] += extra[at : at + tokens] + extra[at + tokens : at + 2 * tokens]
    return jnp.concatenate(pieces, axis=1)


def combine_kernel(
    experts, returned, fwd_routes, bwd_routes, fwd_weights, bwd_weights, bwd_inputs, cot,
    fwd_inputs, gain, fwd_out, bwd_out,
):
    fwd_matrix = weight_matrix(fwd_routes[...], fwd_weights[...], experts)
    combined = weighted_sum(0, returned, fwd_matrix)
    fwd_out[...] = (fwd_inputs[...].astype(F32) + combined).astype(BF)
    bwd_matrix = weight_matrix(bwd_routes[...], bwd_weights[...], experts)
    norm_grad = weighted_sum(1, returned, bwd_matrix)
    norm_scale = gain[...]
    _, values, inv_rms = normalize(bwd_inputs[...], norm_scale)
    scaled = norm_scale * norm_grad
    mean = jnp.mean(values * scaled, axis=-1, keepdims=True)
    bwd_out[...] = (
        cot[...].astype(F32) + inv_rms * scaled - values * (inv_rms * inv_rms * inv_rms) * mean
    ).astype(BF)


def from_behind(value, axis, steps):
    count = lax.axis_size(axis)
    pairs = [(source, (source + steps) % count) for source in range(count)]
    return lax.ppermute(value, axis, pairs)


def body(
    fwd_inputs,
    fwd_routes,
    fwd_weights,
    bwd_inputs,
    bwd_cotangent,
    bwd_routes,
    bwd_weights,
    norm_gain,
    w_gate,
    w_up,
    w_down,
):
    _, tokens, width = fwd_inputs.shape
    local = w_gate.shape[1]
    hidden = w_gate.shape[3]
    group = lax.axis_size("dp") * lax.axis_size("expert")
    experts = local * group
    rows = experts * ROWS
    quarter = width // ROWS
    wide = width + quarter
    bulk = group * ROWS
    vmem = pl.BlockSpec(memory_space=pltpu.VMEM)
    hbm = pl.BlockSpec(memory_space=pltpu.HBM)
    limit = pltpu.CompilerParams(vmem_limit_bytes=65_000_000)
    fwd_routes = fwd_routes[0].T
    bwd_routes = bwd_routes[0].T
    fwd_weights = fwd_weights[0].T
    bwd_weights = bwd_weights[0].T

    def cost(flops, moved):
        return pl.CostEstimate(flops=int(flops), bytes_accessed=int(moved), transcendentals=0)

    def exchange(packed):
        return lax.all_to_all(packed, ("expert", "dp"), split_axis=0, concat_axis=0, tiled=True)

    packed = pl.pallas_call(
        lambda *refs: pack_kernel(experts, *refs),
        out_shape=jax.ShapeDtypeStruct((rows, 3 * wide), BF),
        in_specs=[vmem] * 6,
        out_specs=hbm,
        scratch_shapes=[
            pltpu.VMEM((rows, 3 * wide), BF),
            pltpu.SemaphoreType.DMA((3 * (ROWS + 1),)),
        ],
        compiler_params=limit,
        cost_estimate=cost(9e9, 9e6),
        name="pack",
    )(fwd_inputs[0], bwd_inputs[0], bwd_cotangent[0], fwd_routes, bwd_routes, norm_gain)
    arrived = exchange(packed)
    total = rows + 2 * group
    worked = pl.pallas_call(
        expert_kernel,
        out_shape=jax.ShapeDtypeStruct((rows, 2 * wide), BF),
        in_specs=[vmem] * 4,
        out_specs=vmem,
        scratch_shapes=[
            pltpu.VMEM((3, 2 * group, width), BF),
            pltpu.VMEM((local, width, 2 * hidden), BF),
            pltpu.VMEM((local, total, 2 * hidden), F32),
            pltpu.VMEM((total, local * hidden), F32),
            pltpu.VMEM((local, bulk + group, hidden), BF),
            pltpu.VMEM((local, bulk + group, 2 * hidden), BF),
            pltpu.VMEM((rows, 2 * quarter), BF),
            pltpu.SemaphoreType.DMA((2,)),
        ],
        compiler_params=pltpu.CompilerParams(vmem_limit_bytes=28 * 1024 * 1024),
        cost_estimate=cost(20e9, 22e6),
        name="experts",
    )(
        arrived,
        w_gate[0],
        w_up[0],
        w_down[0].reshape(local * hidden, width),
    )
    returned = exchange(worked)

    one = jax.ShapeDtypeStruct((tokens, width), BF)
    section_out, section_grad = pl.pallas_call(
        lambda *refs: combine_kernel(experts, *refs),
        out_shape=(one, one),
        in_specs=[vmem] * 9,
        out_specs=(vmem, vmem),
        compiler_params=pltpu.CompilerParams(vmem_limit_bytes=16 * 1024 * 1024),
        cost_estimate=cost(4e9, 8e6),
        name="combine",
    )(
        returned,
        fwd_routes,
        bwd_routes,
        fwd_weights,
        bwd_weights,
        bwd_inputs[0],
        bwd_cotangent[0],
        fwd_inputs[0],
        norm_gain,
    )
    next_forward = from_behind(section_out[None], "segment", 1)
    prev_grad = from_behind(section_grad[None], "segment", -1)
    return (next_forward, prev_grad)


def solution(mesh):
    token = P("segment", ("dp", "expert"), None)
    weight = P("segment", ("dp", "expert"), None, None)
    return jax.shard_map(
        body,
        mesh=mesh,
        in_specs=(token,) * 7 + (P("segment", None),) + (weight,) * 3,
        out_specs=(token, token),
        check_vma=False,
    )
```
